256 devices in a mesh: group: 16 (over y_lo, x, core), fsdp: 16 (over y_hi, z).
Axes of the slice: x: 4, y: 4 (y_hi: 2, y_lo: 2; y = y_hi * 2 + y_lo), z: 8, core: 2. Of those that a mesh axis runs over, the one named last changes fastest.
Arguments:
- activations: bfloat16 [16, 6144, 8192], P('group', 'fsdp'), may hold values from -6 to 6
- key_cotangent: bfloat16 [16, 6144, 512], P('group', 'fsdp'), may hold values from -0.079589844 to 0.079589844
- master: float32 [16, 8192, 512], P('group', 'fsdp'), may hold values from -6 to 6
- first_codes: bfloat16 [16, 8192, 512], P('group', 'fsdp'), may hold values from -1 to 1
- first_scales: float32 [16, 8192, 4], P('group', 'fsdp'), may hold values from 0.03 to 0.3
- second_codes: bfloat16 [16, 8192, 512], P('group', 'fsdp'), may hold values from 0.049804688 to 1
- second_scales: float32 [16, 8192, 4], P('group', 'fsdp'), may hold values from 0.2 to 3
- partner: int32 [16], replicated, may hold values from 0 to 15, as said below
Outputs:
- master_out: float32 [16, 8192, 512], P('group', 'fsdp')
- first_codes_out: bfloat16 [16, 8192, 512], P('group', 'fsdp')
- first_scales_out: float32 [16, 8192, 4], P('group', 'fsdp')
- second_codes_out: bfloat16 [16, 8192, 512], P('group', 'fsdp')
- second_scales_out: float32 [16, 8192, 4], P('group', 'fsdp')
The draws below stay inside these ranges and needn't reach their ends.
Inputs may be any that keep to these rules, and one draw needn't show every extreme that they name: partner is a matching: partner[partner[g]] == g and partner[g] != g for every group g.
All inputs are finite; a program needn't handle non-finite values. Where the reference program divides by a largest or mean magnitude, that divisor is 1e-20 or more.
Results may differ from the reference program's by a relative error of at most 0.0085.
Values may be sent and summed in bfloat16 or wider, within the bound.
A program may use at most 128 MiB of HBM per device.

```python
import math
import jax
import jax.numpy as jnp
from jax import lax

D = 8192
KV = 512
NG = 16
TOKENS = 6144
BLOCKS = 4


def draw_partner(key, part):
    order = jax.random.permutation(key, NG).astype(jnp.int32)
    swapped = order.reshape(-1, 2)[:, ::-1].reshape(-1)
    return jnp.zeros((NG,), jnp.int32).at[order].set(swapped)


def raised(drawn, stream_key, source, target, blocks, factor):
    def block_of(axis_at):
        return (jnp.arange(drawn.shape[axis_at]) // (drawn.shape[axis_at] // blocks)).reshape((-1,) + (1,) * (drawn.ndim - 1 - axis_at))

    near = jax.random.permutation(stream_key, blocks)[block_of(target)]
    other_side = (block_of(target) + blocks // 2) % blocks
    return jnp.where((block_of(source) == near) | (block_of(source) == other_side), factor * drawn, drawn)


def level_of(stream_key, shape, shards, low, top_value):
    loudness, own = 1.0, jax.random.fold_in(stream_key, 6)
    for position, shards_of in shards:
        draws = jnp.exp(jax.random.uniform(jax.random.fold_in(own, position), (shards_of,), jnp.float32, low / len(shards), top_value / len(shards)))
        loudness = loudness * jnp.repeat(draws, shape[position] // shards_of).reshape([-1 if axis == position else 1 for axis in range(len(shape))])
    return loudness


def bell_draw(rng, shape, deviation, most, cuts=(), held_as=jnp.bfloat16):
    values = deviation * jax.random.normal(rng, shape, jnp.float32)
    if cuts:
        values = values * level_of(rng, shape, cuts, -0.22, 0.18)
    return jnp.clip(values, -most, most).astype(held_as)


def noise_with(key, shape, spread, bound, split, heavy, held_as=jnp.bfloat16):
    values = spread * jax.random.normal(key, shape, jnp.float32)
    if split:
        values = values * level_of(key, shape, split, -0.22, 0.18)
    return jnp.clip(raised(values, jax.random.fold_in(key, 3), *heavy), -bound, bound).astype(held_as)


def setup_inputs(seed: int = 0) -> dict:
    arg_keys = jax.random.split(jax.random.key(seed), 9)
    activations = noise_with(arg_keys[0], (NG, TOKENS, D), 1.0, 6.0, ((0, 16), (1, 16)), (1, 2, 16, 2.0))
    key_cotangent = bell_draw(arg_keys[1], (NG, TOKENS, KV), 0.0125, 0.079589844, ((0, 16), (1, 16)))
    master = bell_draw(arg_keys[2], (NG, D, KV), 1.0, 6.0, ((0, 16), (1, 16)), jnp.float32)
    first_codes = jnp.clip(jax.random.uniform(arg_keys[3], (NG, D, KV), jnp.float32, -1.0, 1.0) * level_of(arg_keys[3], (NG, D, KV), ((0, 16), (1, 16)), -0.4, 0.0), -1.0, 1.0).astype(jnp.bfloat16)
    first_scales = jnp.clip(jnp.exp(math.log(0.3) - 2.3025852 * jax.random.uniform(arg_keys[4], (NG, D, BLOCKS), jnp.float32) ** level_of(arg_keys[4], (NG, D, BLOCKS), ((0, 16), (1, 16)), -0.2, 0.2)), 0.03, 0.3)
    second_codes = jnp.clip(0.049804688 + 0.9501953 * jax.random.uniform(arg_keys[5], (NG, D, KV), jnp.float32) ** level_of(arg_keys[5], (NG, D, KV), ((0, 16), (1, 16)), -0.2, 0.2), 0.049804688, 1.0).astype(jnp.bfloat16)
    second_scales = jnp.clip(jnp.exp(math.log(3.0) - 2.7080502 * jax.random.uniform(arg_keys[6], (NG, D, BLOCKS), jnp.float32) ** level_of(arg_keys[6], (NG, D, BLOCKS), ((0, 16), (1, 16)), -0.2, 0.2)), 0.2, 3.0)
    partner = draw_partner(jax.random.fold_in(arg_keys[8], 71), 0)
    return dict(activations=activations, key_cotangent=key_cotangent, master=master, first_codes=first_codes, first_scales=first_scales, second_codes=second_codes, second_scales=second_scales, partner=partner)


beta_one = 0.9
beta_two = 0.95
learn_rate = 0.01
decay_rate = 0.1
adam_epsilon = 1e-08
block_epsilon = 1e-06

def quantize(values):
    blocks = values.reshape(values.shape[:-1] + (values.shape[-1] // 128, 128))
    scales = lax.optimization_barrier(jnp.max(jnp.abs(blocks), axis=-1)) + block_epsilon
    codes = (blocks / scales[..., None]).astype(jnp.bfloat16)
    return (codes.reshape(values.shape), scales)

def dequantize(codes, scales):
    blocks = codes.astype(jnp.float32).reshape(codes.shape[:-1] + (codes.shape[-1] // 128, 128))
    return (blocks * scales[..., None]).reshape(codes.shape)

def group_gradient(pair):
    inputs, cotangent = pair
    return jnp.dot(inputs.T, cotangent, preferred_element_type=jnp.float32)

def reference(activations, key_cotangent, master, first_codes, first_scales, second_codes, second_scales, partner):
    grad = lax.map(group_gradient, (activations, key_cotangent))
    first_old = dequantize(first_codes, first_scales)
    second_old = dequantize(second_codes, second_scales)
    first = beta_one * first_old + (1.0 - beta_one) * grad
    second = beta_two * second_old + (1.0 - beta_two) * grad * grad
    updated = master - learn_rate * (first / (jnp.sqrt(second) + adam_epsilon) + decay_rate * master)
    first_codes_mid, first_scales_mid = quantize(first)
    second_codes_mid, second_scales_mid = quantize(second)
    master_out = (updated + updated[partner]) / 2.0
    first_mid = dequantize(first_codes_mid, first_scales_mid)
    second_mid = dequantize(second_codes_mid, second_scales_mid)
    first_avg = (first_mid + first_mid[partner]) / 2.0
    second_avg = (second_mid + second_mid[partner]) / 2.0
    first_codes_out, first_scales_out = quantize(first_avg)
    second_codes_out, second_scales_out = quantize(second_avg)
    return (master_out, first_codes_out, first_scales_out, second_codes_out, second_scales_out)
```

```python
import jax
import jax.numpy as jnp
from jax import lax
from jax.experimental import pallas as pl
from jax.experimental.pallas import tpu as pltpu
from jax.sharding import PartitionSpec as P

beta_one = 0.9
beta_two = 0.95
learn_rate = 0.01
decay_rate = 0.1
adam_epsilon = 1e-08
block_epsilon = 1e-06

NG = 16
NZ = 8
T = 384
W = 512
Q = 4
R = W // Q
NP = 7 * Q
PARTS = 2
PR = W // PARTS
MR = PR // NG
SR = W // NG
BLK = 128
NB = W // BLK
MESH = pl.DeviceIdType.MESH
F32 = jnp.float32
BF16 = jnp.bfloat16


def kernel(
    partner_ref, x_hbm, c_hbm, m_hbm, c1_hbm, c2_hbm, s1_hbm, s2_hbm,
    mo_hbm, c1o_hbm, so1_hbm, c2o_hbm, so2_hbm,
    xv, cv, mv, sbuf, rbuf, ysb, yrb,
    st, st_r, st_b, st_p, sc, sc_all, srow,
    f1, f2, mm, grad, gs, gr0, gr1, gb, gp, mid1, mid2, upd,
    mo, c1o, c2o, so,
    x_sem, in_sem, out_sem, zs_sem, zr_sem, ys_sem, yr_sem,
    ss_sem, sr_sem, cs_sem, cr_sem, ps_sem, pr_sem, gs_sem, gr_sem, hs_sem, hr_sem,
):
    g = lax.axis_index("group")
    f_me = lax.axis_index("fsdp")
    z = f_me % NZ
    yh = f_me // NZ
    y_other = 1 - yh
    up = (g, yh * NZ + (z + 1) % NZ)
    down = (g, yh * NZ + (z + NZ - 1) % NZ)
    across = (g, y_other * NZ + z)

    def member(r):
        return (g + r) % NG

    def x_copy(f):
        cols = pl.ds(pl.multiple_of(f * W, W), W)
        return pltpu.make_async_copy(x_hbm.at[:, cols], xv.at[f], x_sem.at[f])

    def chunk(y, t):
        return y * NZ + t

    far = (z + 4) % NZ
    first_chunks = [
        chunk(y_other, far), chunk(yh, far),
        chunk(yh, (z + 3) % NZ), chunk(y_other, (z + 5) % NZ),
    ]
    c_in = pltpu.make_async_copy(c_hbm, cv, in_sem.at[0])
    c_in.start()
    for f in first_chunks:
        x_copy(f).start()
    state_in = [
        pltpu.make_async_copy(m_hbm, mv, in_sem.at[1]),
        pltpu.make_async_copy(c1_hbm, st.at[:, 1], in_sem.at[2]),
        pltpu.make_async_copy(c2_hbm, st.at[:, 2], in_sem.at[3]),
        pltpu.make_async_copy(s1_hbm, sc.at[pl.ds(0, NB)], in_sem.at[4]),
        pltpu.make_async_copy(s2_hbm, sc.at[pl.ds(NB, NB)], in_sem.at[5]),
    ]
    rest = [chunk(yh, (z + 5) % NZ), chunk(y_other, (z + 3) % NZ)]
    for d in (2, 6, 1, 7, 0):
        rest += [chunk(y_other, (z + d) % NZ), chunk(yh, (z + d) % NZ)]
    for f in rest[:2]:
        x_copy(f).start()
    for c in state_in:
        c.start()
    for f in rest[2:]:
        x_copy(f).start()

    barrier = pltpu.get_barrier_semaphore()
    for d in (up, down, across):
        pl.semaphore_signal(barrier, inc=1, device_id=d, device_id_type=MESH)

    def greet(r, _):
        pl.semaphore_signal(barrier, inc=1, device_id=(member(r), f_me), device_id_type=MESH)
        return 0

    lax.fori_loop(1, NG, greet, 0)

    def partial_grad(f, q):
        cols = pl.ds(pl.multiple_of(q * R, R), R)
        return lax.dot_general(
            xv[f, :, cols], cv[...], (((0,), (0,)), ((), ())), preferred_element_type=F32
        )

    def ring_copy(way, n):
        return pltpu.make_async_remote_copy(
            src_ref=sbuf.at[way, n], dst_ref=rbuf.at[way, n],
            send_sem=zs_sem.at[way, n], recv_sem=zr_sem.at[way, n],
            device_id=(up, down)[way], device_id_type=MESH,
        )

    def ring_piece(way, n, fresh):
        m = n + Q
        step, p = m // (2 * Q), m % (2 * Q)
        q, half = p % Q, p // Q
        d = 4 - step
        last = step // 3
        if way == 0:
            kind = half + (1 - 2 * half) * (1 - last)
            t = (z + d) % NZ
            prev = n - 2 * Q + last * (Q - 2 * Q * half)
        else:
            kind = half
            t = (z + NZ - d) % NZ
            prev = n - 2 * Q
        y = yh * kind + y_other * (1 - kind)
        f = chunk(y, t)
        total = partial_grad(f, q)
        if not fresh:
            ring_copy(way, prev).wait_recv()
            total = total + rbuf[way, prev].astype(F32)
        sbuf[way, n] = total.astype(BF16)
        ring_copy(way, n).start()

    def fresh_step(n, _):
        ring_piece(0, n, True)
        ring_piece(1, n, True)
        return 0

    def ring_step(n, _):
        ring_piece(0, n, False)
        ring_piece(1, n, False)
        return 0

    c_in.wait()
    x_copy(first_chunks[0]).wait()
    x_copy(first_chunks[1]).wait()
    pl.semaphore_wait(barrier, NG + 2)
    lax.fori_loop(0, Q, fresh_step, 0)
    x_copy(first_chunks[2]).wait()
    x_copy(first_chunks[3]).wait()
    lax.fori_loop(Q, 2 * Q, fresh_step, 0)

    for c in state_in:
        c.wait()
    for f in rest:
        x_copy(f).wait()

    def to_bf16(j, _):
        st[j, 0] = mv[j].astype(BF16)
        return 0

    lax.fori_loop(0, NG, to_bf16, 0)

    def spread_copy(r, src, dst, s_sem, r_sem):
        return pltpu.make_async_remote_copy(
            src_ref=src, dst_ref=dst, send_sem=s_sem, recv_sem=r_sem,
            device_id=(member(r), f_me), device_id_type=MESH,
        )

    def state_out(r):
        return spread_copy(r, st.at[member(r)], st_r.at[g], ss_sem.at[r], sr_sem.at[r])

    def scale_out(r):
        return spread_copy(r, sc, sc_all.at[g], cs_sem.at[r], cr_sem.at[r])

    def state_back(r):
        return spread_copy(r, st_b.at[member(r)], st_p.at[g], ps_sem.at[r], pr_sem.at[r])

    def each_member(fn):
        def body(r, _):
            fn(r)
            return 0

        lax.fori_loop(1, NG, body, 0)

    def start_state(r):
        state_out(r).start()
        scale_out(r).start()

    each_member(start_state)
    st_r[g] = st[g]
    sc_all[g] = sc[...]

    lax.fori_loop(2 * Q, 4 * Q, ring_step, 0)

    def state_arrived(r):
        state_out(r).wait_recv()
        scale_out(r).wait_recv()

    each_member(state_arrived)

    def select_state(h, _):
        st_b[h] = st_r[partner_ref[h]]
        return 0

    lax.fori_loop(0, NG, select_state, 0)
    each_member(lambda r: state_back(r).start())
    st_p[g] = st_b[g]

    lax.fori_loop(4 * Q, 5 * Q, ring_step, 0)

    each_member(lambda r: state_back(r).wait_recv())
    srow[0] = jnp.transpose(sc[...])
    srow[1] = jnp.transpose(sc_all[partner_ref[g]])

    def prepare(j, _):
        rows = pl.ds(pl.multiple_of(j * SR, SR), SR)
        own_s, other_s = srow[0, rows, :], srow[1, rows, :]
        for b in range(NB):
            lanes = slice(b * BLK, (b + 1) * BLK)
            for who, buf, s in ((0, st, own_s), (1, st_p, other_s)):
                f1[who, rows, lanes] = beta_one * (buf[j, 1, :, lanes].astype(F32) * s[:, b : b + 1])
                f2[who, rows, lanes] = beta_two * (
                    buf[j, 2, :, lanes].astype(F32) * s[:, NB + b : NB + b + 1]
                )
        mm[rows, :] = (0.5 * (1.0 - learn_rate * decay_rate)) * (mv[j] + st_p[j, 0].astype(F32))
        return 0

    lax.fori_loop(0, NG, prepare, 0)

    lax.fori_loop(5 * Q, NP, ring_step, 0)

    def across_copy(q):
        return pltpu.make_async_remote_copy(
            src_ref=ysb.at[q], dst_ref=yrb.at[q], send_sem=ys_sem.at[q], recv_sem=yr_sem.at[q],
            device_id=across, device_id_type=MESH,
        )

    def plane_sum(y, n, q):
        total = partial_grad(chunk(y, z), q)
        ring_copy(0, n).wait_recv()
        ring_copy(1, n).wait_recv()
        return total + rbuf[0, n].astype(F32) + rbuf[1, n].astype(F32)

    def other_plane(q, _):
        ysb[q] = plane_sum(y_other, 5 * Q + q, q).astype(BF16)
        across_copy(q).start()
        return 0

    lax.fori_loop(0, Q, other_plane, 0)

    gr = (gr0, gr1)

    def grad_out(k, r):
        return spread_copy(r, gs.at[k, member(r)], gr[k].at[g], gs_sem.at[k, r], gr_sem.at[k, r])

    def grad_back(k, r):
        return spread_copy(r, gb.at[k, member(r)], gp.at[k, g], hs_sem.at[k, r], hr_sem.at[k, r])

    def own_plane(q, _):
        total = plane_sum(yh, 6 * Q + q, q)
        across_copy(q).wait_recv()
        total = total + yrb[q].astype(F32)
        grad[pl.ds(pl.multiple_of(q * R, R), R), :] = total
        k = q // (Q // PARTS)
        first = (q % (Q // PARTS)) * (R // MR)
        gs[k, pl.ds(first, R // MR)] = total.astype(BF16).reshape(R // MR, MR, W)
        return 0

    def moments(value, who, rows, lanes):
        first = f1[who, rows, lanes] + (1.0 - beta_one) * value
        second = f2[who, rows, lanes] + (1.0 - beta_two) * value * value
        step = first / (jnp.sqrt(second) + adam_epsilon)
        return rounded(first), rounded(second), step

    def quantize(values):
        scale = jnp.max(jnp.abs(values), axis=-1, keepdims=True) + block_epsilon
        return (values * (1.0 / scale)).astype(BF16), scale

    def rounded(values):
        codes, scale = quantize(values)
        return codes.astype(F32) * scale

    def own_update(k):
        def body(i, _):
            rows = pl.ds(pl.multiple_of(k * PR + i * MR, MR), MR)
            for b in range(NB):
                lanes = slice(b * BLK, (b + 1) * BLK)
                one, two, step = moments(grad[rows, lanes], 0, rows, lanes)
                mid1[rows, lanes] = one
                mid2[rows, lanes] = two
                upd[rows, lanes] = mm[rows, lanes] - (0.5 * learn_rate) * step
            return 0

        lax.fori_loop(0, NG, body, 0)

    def final_update(k):
        def body(i, _):
            rows = pl.ds(pl.multiple_of(k * PR + i * MR, MR), MR)
            scales = []
            for b in range(NB):
                lanes = slice(b * BLK, (b + 1) * BLK)
                one, two, step = moments(gp[k, i, :, lanes].astype(F32), 1, rows, lanes)
                mo[rows, lanes] = upd[rows, lanes] - (0.5 * learn_rate) * step
                codes, scale = quantize(0.5 * (mid1[rows, lanes] + one))
                c1o[rows, lanes] = codes
                srow[0, rows, b : b + 1] = scale
                codes, scale = quantize(0.5 * (mid2[rows, lanes] + two))
                c2o[rows, lanes] = codes
                srow[0, rows, NB + b : NB + b + 1] = scale
            return 0

        lax.fori_loop(0, NG, body, 0)

    def start_grads(k):
        each_member(lambda r: grad_out(k, r).start())
        gr[k][g] = gs[k, g]

    def pass_grads(k):
        each_member(lambda r: grad_out(k, r).wait_recv())

        def select(h, _):
            gb[k, h] = gr[k][partner_ref[h]]
            return 0

        lax.fori_loop(0, NG, select, 0)
        each_member(lambda r: grad_back(k, r).start())
        gp[k, g] = gb[k, g]

    def outs(k):
        rows = pl.ds(k * PR, PR)
        return [
            pltpu.make_async_copy(mo.at[rows], mo_hbm.at[rows], out_sem.at[k, 0]),
            pltpu.make_async_copy(c1o.at[rows], c1o_hbm.at[rows], out_sem.at[k, 1]),
            pltpu.make_async_copy(c2o.at[rows], c2o_hbm.at[rows], out_sem.at[k, 2]),
        ]

    lax.fori_loop(0, Q // PARTS, own_plane, 0)
    start_grads(0)
    lax.fori_loop(Q // PARTS, Q, own_plane, 0)
    start_grads(1)
    own_update(0)
    pass_grads(0)
    own_update(1)
    pass_grads(1)
    for k in range(PARTS):
        each_member(lambda r: grad_back(k, r).wait_recv())
        final_update(k)
        for c in outs(k):
            c.start()
    so[...] = jnp.transpose(srow[0])
    scale_copies = [
        pltpu.make_async_copy(so.at[pl.ds(0, NB)], so1_hbm, in_sem.at[4]),
        pltpu.make_async_copy(so.at[pl.ds(NB, NB)], so2_hbm, in_sem.at[5]),
    ]
    for c in scale_copies:
        c.start()

    def ring_sent(n, _):
        ring_copy(0, n).wait_send()
        ring_copy(1, n).wait_send()
        return 0

    lax.fori_loop(0, NP, ring_sent, 0)

    def across_sent(q, _):
        across_copy(q).wait_send()
        return 0

    lax.fori_loop(0, Q, across_sent, 0)

    def all_sent(r):
        state_out(r).wait_send()
        scale_out(r).wait_send()
        state_back(r).wait_send()
        for k in range(PARTS):
            grad_out(k, r).wait_send()
            grad_back(k, r).wait_send()

    each_member(all_sent)
    for k in range(PARTS):
        for c in outs(k):
            c.wait()
    for c in scale_copies:
        c.wait()


def per_device(x, c, master, c1, s1, c2, s2, partner):
    anywhere = pl.BlockSpec(memory_space=pl.ANY)
    vm, dma = pltpu.VMEM, pltpu.SemaphoreType.DMA
    mo, c1o, so1, c2o, so2 = pl.pallas_call(
        kernel,
        out_shape=(
            jax.ShapeDtypeStruct((W, W), F32),
            jax.ShapeDtypeStruct((W, W), BF16),
            jax.ShapeDtypeStruct((NB, W), F32),
            jax.ShapeDtypeStruct((W, W), BF16),
            jax.ShapeDtypeStruct((NB, W), F32),
        ),
        in_specs=[pl.BlockSpec(memory_space=pltpu.SMEM)] + [anywhere] * 7,
        out_specs=[anywhere] * 5,
        scratch_shapes=[
            vm((2 * NZ, T, W), BF16), vm((T, W), BF16), vm((NG, SR, W), F32),
            vm((2, NP, R, W), BF16), vm((2, NP, R, W), BF16), vm((Q, R, W), BF16), vm((Q, R, W), BF16),
            vm((NG, 3, SR, W), BF16), vm((NG, 3, SR, W), BF16), vm((NG, 3, SR, W), BF16),
            vm((NG, 3, SR, W), BF16), vm((2 * NB, W), F32), vm((NG, 2 * NB, W), F32),
            vm((2, W, 2 * NB), F32),
            vm((2, W, W), F32), vm((2, W, W), F32), vm((W, W), F32), vm((W, W), F32),
            vm((PARTS, NG, MR, W), BF16), vm((NG, MR, W), BF16), vm((NG, MR, W), BF16),
            vm((PARTS, NG, MR, W), BF16), vm((PARTS, NG, MR, W), BF16),
            vm((W, W), F32), vm((W, W), F32), vm((W, W), F32),
            vm((W, W), F32), vm((W, W), BF16), vm((W, W), BF16), vm((2 * NB, W), F32),
            dma((2 * NZ,)), dma((6,)), dma((PARTS, 3)),
            dma((2, NP)), dma((2, NP)), dma((Q,)), dma((Q,)),
            dma((NG,)), dma((NG,)), dma((NG,)), dma((NG,)), dma((NG,)), dma((NG,)),
            dma((PARTS, NG)), dma((PARTS, NG)), dma((PARTS, NG)), dma((PARTS, NG)),
        ],
        compiler_params=pltpu.CompilerParams(
            collective_id=0, has_side_effects=True, vmem_limit_bytes=67043328
        ),
    )(
        partner, x[0], c[0], master.reshape(NG, SR, W), c1.reshape(NG, SR, W),
        c2.reshape(NG, SR, W), s1[0].T, s2[0].T,
    )
    return (mo[None], c1o[None], so1.T[None], c2o[None], so2.T[None])


def solution(mesh):
    rows = P("group", "fsdp", None)
    return jax.shard_map(
        per_device, mesh=mesh, in_specs=(rows,) * 7 + (P(),), out_specs=(rows,) * 5, check_vma=False
    )
```

```python
import jax
import jax.numpy as jnp
from jax import lax
from jax.experimental import pallas as pl
from jax.experimental.pallas import tpu as pltpu
from jax.sharding import PartitionSpec as P

beta_one = 0.9
beta_two = 0.95
learn_rate = 0.01
decay_rate = 0.1
adam_epsilon = 1e-08
block_epsilon = 1e-06

NG = 16
NZ = 8
T = 384
W = 512
Q = 4
R = W // Q
NP = 7 * Q
MR = 2 * R // NG
HW = W // 2
TR = 32
SR = W // NG
BLK = 128
NB = W // BLK
MESH = pl.DeviceIdType.MESH
F32 = jnp.float32
BF16 = jnp.bfloat16


def kernel(
    partner_ref, x_hbm, c_hbm, m_hbm, c1_hbm, c2_hbm, s1_hbm, s2_hbm,
    mo_hbm, c1o_hbm, so1_hbm, c2o_hbm, so2_hbm,
    xv, cv, mv, sbuf, rbuf, ysb, yrb,
    st, st_r, st_b, st_p, sc, sc_all, srow,
    f1, f2, mm, grad, gs, gr0, gr1, gr2, gr3, gb, gp, mid1, mid2, upd,
    mo, c1o, c2o, so,
    x_sem, xf_sem, in_sem, out_sem, zs_sem, zr_sem, ys_sem, yr_sem,
    ss_sem, sr_sem, cs_sem, cr_sem, ps_sem, pr_sem, gs_sem, gr_sem, hs_sem, hr_sem,
):
    g = lax.axis_index("group")
    f_me = lax.axis_index("fsdp")
    z = f_me % NZ
    yh = f_me // NZ
    y_other = 1 - yh
    up = (g, yh * NZ + (z + 1) % NZ)
    down = (g, yh * NZ + (z + NZ - 1) % NZ)
    across = (g, y_other * NZ + z)

    def member(r):
        return (g + r) % NG

    def x_copy(f):
        cols = pl.ds(pl.multiple_of(f * W, W), W)
        return pltpu.make_async_copy(x_hbm.at[:, cols], xv.at[f], x_sem.at[f])

    def chunk(y, t):
        return y * NZ + t

    far = (z + 4) % NZ
    first_chunks = [
        chunk(y_other, far), chunk(yh, far),
        chunk(yh, (z + 3) % NZ), chunk(y_other, (z + 5) % NZ),
    ]
    c_in = pltpu.make_async_copy(c_hbm, cv, in_sem.at[0])
    c_in.start()

    def first_copy(way, q):
        f = first_chunks[way]
        cols = pl.ds(pl.multiple_of(f * W + q * R, R), R)
        mine = pl.ds(pl.multiple_of(q * R, R), R)
        return pltpu.make_async_copy(x_hbm.at[:, cols], xv.at[f, :, mine], xf_sem.at[way, q])

    first_copy(0, 0).start()
    first_copy(1, 0).start()
    state_in = [
        pltpu.make_async_copy(m_hbm, mv, in_sem.at[1]),
        pltpu.make_async_copy(c1_hbm, st.at[:, 1], in_sem.at[2]),
        pltpu.make_async_copy(c2_hbm, st.at[:, 2], in_sem.at[3]),
        pltpu.make_async_copy(s1_hbm, sc.at[pl.ds(0, NB)], in_sem.at[4]),
        pltpu.make_async_copy(s2_hbm, sc.at[pl.ds(NB, NB)], in_sem.at[5]),
    ]
    rest = [chunk(yh, (z + 5) % NZ), chunk(y_other, (z + 3) % NZ)]
    for d in (2, 6, 1, 7, 0):
        rest += [chunk(y_other, (z + d) % NZ), chunk(yh, (z + d) % NZ)]

    barrier = pltpu.get_barrier_semaphore()
    for d in (up, down, across):
        pl.semaphore_signal(barrier, inc=1, device_id=d, device_id_type=MESH)

    def greet(r, _):
        pl.semaphore_signal(barrier, inc=1, device_id=(member(r), f_me), device_id_type=MESH)
        return 0

    lax.fori_loop(1, NG, greet, 0)
    for q in range(1, Q):
        first_copy(0, q).start()
        first_copy(1, q).start()
    for f in first_chunks[2:] + rest[:2]:
        x_copy(f).start()
    for c in state_in:
        c.start()
    for f in rest[2:]:
        x_copy(f).start()

    def partial_grad(f, q):
        cols = pl.ds(pl.multiple_of(q * R, R), R)
        return lax.dot_general(
            xv[f, :, cols], cv[...], (((0,), (0,)), ((), ())), preferred_element_type=F32
        )

    def ring_copy(way, n):
        return pltpu.make_async_remote_copy(
            src_ref=sbuf.at[way, n], dst_ref=rbuf.at[way, n],
            send_sem=zs_sem.at[way, n], recv_sem=zr_sem.at[way, n],
            device_id=(up, down)[way], device_id_type=MESH,
        )

    def ring_piece(way, n, fresh):
        m = n + Q
        step, p = m // (2 * Q), m % (2 * Q)
        q, half = p % Q, p // Q
        d = 4 - step
        last = step // 3
        if way == 0:
            kind = half + (1 - 2 * half) * (1 - last)
            t = (z + d) % NZ
            prev = n - 2 * Q + last * (Q - 2 * Q * half)
        else:
            kind = half
            t = (z + NZ - d) % NZ
            prev = n - 2 * Q
        y = yh * kind + y_other * (1 - kind)
        f = chunk(y, t)
        total = partial_grad(f, q)
        if not fresh:
            ring_copy(way, prev).wait_recv()
            total = total + rbuf[way, prev].astype(F32)
        sbuf[way, n] = total.astype(BF16)
        ring_copy(way, n).start()

    def first_step(n, _):
        first_copy(0, n).wait()
        first_copy(1, n).wait()
        return fresh_step(n, 0)

    def fresh_step(n, _):
        ring_piece(0, n, True)
        ring_piece(1, n, True)
        return 0

    def ring_step(n, _):
        ring_piece(0, n, False)
        ring_piece(1, n, False)
        return 0

    c_in.wait()
    pl.semaphore_wait(barrier, NG + 2)
    lax.fori_loop(0, Q, first_step, 0)
    x_copy(first_chunks[2]).wait()
    x_copy(first_chunks[3]).wait()
    lax.fori_loop(Q, 2 * Q, fresh_step, 0)

    for c in state_in:
        c.wait()
    for f in rest:
        x_copy(f).wait()

    def to_bf16(j, _):
        st[j, 0] = mv[j].astype(BF16)
        return 0

    lax.fori_loop(0, NG, to_bf16, 0)

    def spread_copy(r, src, dst, s_sem, r_sem):
        return pltpu.make_async_remote_copy(
            src_ref=src, dst_ref=dst, send_sem=s_sem, recv_sem=r_sem,
            device_id=(member(r), f_me), device_id_type=MESH,
        )

    def state_out(r):
        return spread_copy(r, st.at[member(r)], st_r.at[g], ss_sem.at[r], sr_sem.at[r])

    def scale_out(r):
        return spread_copy(r, sc, sc_all.at[g], cs_sem.at[r], cr_sem.at[r])

    def state_back(r):
        return spread_copy(r, st_b.at[member(r)], st_p.at[g], ps_sem.at[r], pr_sem.at[r])

    def each_member(fn):
        def body(r, _):
            fn(r)
            return 0

        lax.fori_loop(1, NG, body, 0)

    def start_state(r):
        state_out(r).start()
        scale_out(r).start()

    each_member(start_state)
    st_r[g] = st[g]
    sc_all[g] = sc[...]

    lax.fori_loop(2 * Q, 4 * Q, ring_step, 0)

    def state_arrived(r):
        state_out(r).wait_recv()
        scale_out(r).wait_recv()

    each_member(state_arrived)

    def select_state(h, _):
        st_b[h] = st_r[partner_ref[h]]
        return 0

    lax.fori_loop(0, NG, select_state, 0)
    each_member(lambda r: state_back(r).start())
    st_p[g] = st_b[g]

    lax.fori_loop(4 * Q, 5 * Q, ring_step, 0)

    each_member(lambda r: state_back(r).wait_recv())
    srow[0] = jnp.transpose(sc[...])
    srow[1] = jnp.transpose(sc_all[partner_ref[g]])

    def prepare(j, _):
        rows = pl.ds(pl.multiple_of(j * SR, SR), SR)
        own_s, other_s = srow[0, rows, :], srow[1, rows, :]
        for b in range(NB):
            lanes = slice(b * BLK, (b + 1) * BLK)
            for who, buf, s in ((0, st, own_s), (1, st_p, other_s)):
                f1[who, rows, lanes] = beta_one * (buf[j, 1, :, lanes].astype(F32) * s[:, b : b + 1])
                f2[who, rows, lanes] = beta_two * (
                    buf[j, 2, :, lanes].astype(F32) * s[:, NB + b : NB + b + 1]
                )
        mm[rows, :] = (0.5 * (1.0 - learn_rate * decay_rate)) * (mv[j] + st_p[j, 0].astype(F32))
        return 0

    lax.fori_loop(0, NG, prepare, 0)

    lax.fori_loop(5 * Q, NP, ring_step, 0)

    def across_copy(q):
        return pltpu.make_async_remote_copy(
            src_ref=ysb.at[q], dst_ref=yrb.at[q], send_sem=ys_sem.at[q], recv_sem=yr_sem.at[q],
            device_id=across, device_id_type=MESH,
        )

    def plane_sum(y, n, q):
        total = partial_grad(chunk(y, z), q)
        ring_copy(0, n).wait_recv()
        ring_copy(1, n).wait_recv()
        return total + rbuf[0, n].astype(F32) + rbuf[1, n].astype(F32)

    def other_plane(q, _):
        ysb[q] = plane_sum(y_other, 5 * Q + q, q).astype(BF16)
        across_copy(q).start()
        return 0

    lax.fori_loop(0, Q, other_plane, 0)

    gr = (gr0, gr1, gr2, gr3)

    def grad_out(k, r):
        return spread_copy(r, gs.at[k, member(r)], gr[k].at[g], gs_sem.at[k, r], gr_sem.at[k, r])

    def grad_back(k, r):
        return spread_copy(r, gb.at[k, member(r)], gp.at[k, g], hs_sem.at[k, r], hr_sem.at[k, r])

    def own_plane(q):
        total = plane_sum(yh, 6 * Q + q, q)
        across_copy(q).wait_recv()
        total = total + yrb[q].astype(F32)
        grad[q * R : (q + 1) * R, :] = total
        sent = total.astype(BF16)
        for j in range(NG):
            i, h = j // 2, j % 2
            gs[q, j] = sent[i * MR : (i + 1) * MR, h * HW : (h + 1) * HW]

    def moments(value, who, rows, lanes):
        first = f1[who, rows, lanes] + (1.0 - beta_one) * value
        second = f2[who, rows, lanes] + (1.0 - beta_two) * value * value
        step = first / (jnp.sqrt(second) + adam_epsilon)
        return rounded(first), rounded(second), step

    def quantize(values):
        scale = jnp.max(jnp.abs(values), axis=-1, keepdims=True) + block_epsilon
        return (values * (1.0 / scale)).astype(BF16), scale

    def rounded(values):
        codes, scale = quantize(values)
        return codes.astype(F32) * scale

    def own_update(k):
        def body(i, _):
            rows = pl.ds(pl.multiple_of(k * R + i * TR, TR), TR)
            for b in range(NB):
                lanes = slice(b * BLK, (b + 1) * BLK)
                one, two, step = moments(grad[rows, lanes], 0, rows, lanes)
                mid1[rows, lanes] = one
                mid2[rows, lanes] = two
                upd[rows, lanes] = mm[rows, lanes] - (0.5 * learn_rate) * step
            return 0

        lax.fori_loop(0, R // TR, body, 0)

    def final_update(k):
        def body(i, _):
            rows = pl.ds(pl.multiple_of(k * R + i * TR, TR), TR)
            for b in range(NB):
                lanes = slice(b * BLK, (b + 1) * BLK)
                h, first = b // 2, (b % 2) * BLK
                other = jnp.concatenate(
                    [
                        gp[k, 2 * (i * (TR // MR) + u) + h, :, first : first + BLK]
                        for u in range(TR // MR)
                    ],
                    axis=0,
                )
                one, two, step = moments(other.astype(F32), 1, rows, lanes)
                mo[rows, lanes] = upd[rows, lanes] - (0.5 * learn_rate) * step
                codes, scale = quantize(0.5 * (mid1[rows, lanes] + one))
                c1o[rows, lanes] = codes
                srow[0, rows, b : b + 1] = scale
                codes, scale = quantize(0.5 * (mid2[rows, lanes] + two))
                c2o[rows, lanes] = codes
                srow[0, rows, NB + b : NB + b + 1] = scale
            return 0

        lax.fori_loop(0, R // TR, body, 0)

    def start_grads(k):
        each_member(lambda r: grad_out(k, r).start())
        gr[k][g] = gs[k, g]

    def pass_grads(k):
        each_member(lambda r: grad_out(k, r).wait_recv())

        def select(h, _):
            gb[k, h] = gr[k][partner_ref[h]]
            return 0

        lax.fori_loop(0, NG, select, 0)
        each_member(lambda r: grad_back(k, r).start())
        gp[k, g] = gb[k, g]

    def outs(k):
        rows = pl.ds(k * R, R)
        return [
            pltpu.make_async_copy(mo.at[rows], mo_hbm.at[rows], out_sem.at[k, 0]),
            pltpu.make_async_copy(c1o.at[rows], c1o_hbm.at[rows], out_sem.at[k, 1]),
            pltpu.make_async_copy(c2o.at[rows], c2o_hbm.at[rows], out_sem.at[k, 2]),
        ]

    def finish(k):
        each_member(lambda r: grad_back(k, r).wait_recv())
        final_update(k)
        for c in outs(k):
            c.start()

    def ring_sent(n, _):
        ring_copy(0, n).wait_send()
        ring_copy(1, n).wait_send()
        return 0

    def across_sent(q, _):
        across_copy(q).wait_send()
        return 0

    def early_sent(r):
        state_out(r).wait_send()
        scale_out(r).wait_send()
        state_back(r).wait_send()

    for k in range(Q):
        own_plane(k)
        start_grads(k)
        own_update(k)
        if k >= 1:
            pass_grads(k - 1)
        if k >= 2:
            finish(k - 2)
    each_member(early_sent)
    lax.fori_loop(0, Q, across_sent, 0)
    pass_grads(Q - 1)
    finish(Q - 2)
    lax.fori_loop(0, NP, ring_sent, 0)
    finish(Q - 1)
    so[...] = jnp.transpose(srow[0])
    scale_copies = [
        pltpu.make_async_copy(so.at[pl.ds(0, NB)], so1_hbm, in_sem.at[4]),
        pltpu.make_async_copy(so.at[pl.ds(NB, NB)], so2_hbm, in_sem.at[5]),
    ]
    for c in scale_copies:
        c.start()

    def grads_sent(r):
        for k in range(Q):
            grad_out(k, r).wait_send()
            grad_back(k, r).wait_send()

    each_member(grads_sent)
    for k in range(Q):
        for c in outs(k):
            c.wait()
    for c in scale_copies:
        c.wait()


def store_kernel(*refs):
    ins, outs, sems = refs[:5], refs[5:10], refs[10]
    copies = [pltpu.make_async_copy(a, b, sems.at[i]) for i, (a, b) in enumerate(zip(ins, outs))]
    for c in copies:
        c.start()
    for c in copies:
        c.wait()


def per_device(x, c, master, c1, s1, c2, s2, partner):
    anywhere = pl.BlockSpec(memory_space=pl.ANY)
    in_hbm = pl.BlockSpec(memory_space=pltpu.HBM)
    vm, dma = pltpu.VMEM, pltpu.SemaphoreType.DMA
    results = pl.pallas_call(
        kernel,
        out_shape=(
            jax.ShapeDtypeStruct((W, W), F32),
            jax.ShapeDtypeStruct((W, W), BF16),
            jax.ShapeDtypeStruct((NB, W), F32),
            jax.ShapeDtypeStruct((W, W), BF16),
            jax.ShapeDtypeStruct((NB, W), F32),
        ),
        in_specs=[pl.BlockSpec(memory_space=pltpu.SMEM)] + [in_hbm] * 7,
        out_specs=[anywhere] * 5,
        scratch_shapes=[
            vm((2 * NZ, T, W), BF16), vm((T, W), BF16), vm((NG, SR, W), F32),
            vm((2, NP, R, W), BF16), vm((2, NP, R, W), BF16), vm((Q, R, W), BF16), vm((Q, R, W), BF16),
            vm((NG, 3, SR, W), BF16), vm((NG, 3, SR, W), BF16), vm((NG, 3, SR, W), BF16),
            vm((NG, 3, SR, W), BF16), vm((2 * NB, W), F32), vm((NG, 2 * NB, W), F32),
            vm((2, W, 2 * NB), F32),
            vm((2, W, W), F32), vm((2, W, W), F32), vm((W, W), F32), vm((W, W), F32),
            vm((Q, NG, MR, HW), BF16), *(vm((NG, MR, HW), BF16) for _ in range(4)),
            vm((Q, NG, MR, HW), BF16), vm((Q, NG, MR, HW), BF16),
            vm((W, W), F32), vm((W, W), F32), vm((W, W), F32),
            vm((W, W), F32), vm((W, W), BF16), vm((W, W), BF16), vm((2 * NB, W), F32),
            dma((2 * NZ,)), dma((2, Q)), dma((6,)), dma((Q, 3)),
            dma((2, NP)), dma((2, NP)), dma((Q,)), dma((Q,)),
            dma((NG,)), dma((NG,)), dma((NG,)), dma((NG,)), dma((NG,)), dma((NG,)),
            dma((Q, NG)), dma((Q, NG)), dma((Q, NG)), dma((Q, NG)),
        ],
        compiler_params=pltpu.CompilerParams(
            collective_id=0, has_side_effects=True, vmem_limit_bytes=46 << 20
        ),
    )(
        partner, *(
            pltpu.with_memory_space_constraint(a, pltpu.HBM)
            for a in (
                x[0], c[0], master.reshape(NG, SR, W), c1.reshape(NG, SR, W),
                c2.reshape(NG, SR, W), s1[0].T, s2[0].T,
            )
        )
    )
    mo, c1o, so1, c2o, so2 = pl.pallas_call(
        store_kernel,
        out_shape=tuple(jax.ShapeDtypeStruct(a.shape, a.dtype) for a in results),
        in_specs=[anywhere] * 5,
        out_specs=[in_hbm] * 5,
        scratch_shapes=[dma((5,))],
        compiler_params=pltpu.CompilerParams(vmem_limit_bytes=1 << 20),
    )(*results)
    return (mo[None], c1o[None], so1.T[None], c2o[None], so2.T[None])


def solution(mesh):
    rows = P("group", "fsdp", None)
    return jax.shard_map(
        per_device, mesh=mesh, in_specs=(rows,) * 7 + (P(),), out_specs=(rows,) * 5, check_vma=False
    )
```

```python
import jax
import jax.numpy as jnp
from jax import lax
from jax.experimental import pallas as pl
from jax.experimental.pallas import tpu as pltpu
from jax.sharding import PartitionSpec as P

beta_one = 0.9
beta_two = 0.95
learn_rate = 0.01
decay_rate = 0.1
adam_epsilon = 1e-08
block_epsilon = 1e-06

NG = 16
NZ = 8
T = 384
W = 512
Q = 4
R = W // Q
QB = Q - 1
RB = 64
RO = R - RB
SLOTS = 8 * Q
MR = 2 * R // NG
HW = W // 2
TR = 32
SR = W // NG
BLK = 128
NB = W // BLK
MESH = pl.DeviceIdType.MESH
F32 = jnp.float32
BF16 = jnp.bfloat16


def kernel(
    partner_ref, x_hbm, c_hbm, m_hbm, c1_hbm, c2_hbm, s1_hbm, s2_hbm,
    mo_hbm, c1o_hbm, so1_hbm, c2o_hbm, so2_hbm,
    xv, cv, mv, sbuf, rbuf, ysb, yrb, ybs, ybr,
    st, st_r, st_b, st_p, sc, sc_all, srow,
    f1, f2, mm, grad, gs, gr0, gr1, gr2, gr3, gb, gp, mid1, mid2, upd,
    mo, c1o, c2o, so,
    x_sem, xf_sem, in_sem, out_sem, zs_sem, zr_sem, ys_sem, yr_sem, bs_sem, br_sem,
    ss_sem, sr_sem, cs_sem, cr_sem, ps_sem, pr_sem, gs_sem, gr_sem, hs_sem, hr_sem,
):
    g = lax.axis_index("group")
    f_me = lax.axis_index("fsdp")
    z = f_me % NZ
    yh = f_me // NZ
    y_other = 1 - yh
    up = (g, yh * NZ + (z + 1) % NZ)
    down = (g, yh * NZ + (z + NZ - 1) % NZ)
    across = (g, y_other * NZ + z)

    def member(r):
        return (g + r) % NG

    def x_copy(f):
        cols = pl.ds(pl.multiple_of(f * W, W), W)
        return pltpu.make_async_copy(x_hbm.at[:, cols], xv.at[f], x_sem.at[f])

    def chunk(y, t):
        return y * NZ + t

    far = (z + 4) % NZ
    first_chunks = [
        chunk(y_other, far), chunk(yh, far),
        chunk(yh, (z + 3) % NZ), chunk(y_other, (z + 5) % NZ),
    ]
    c_in = pltpu.make_async_copy(c_hbm, cv, in_sem.at[0])
    c_in.start()

    def first_copy(way, q):
        f = first_chunks[way]
        cols = pl.ds(pl.multiple_of(f * W + q * R, R), R)
        mine = pl.ds(pl.multiple_of(q * R, R), R)
        return pltpu.make_async_copy(x_hbm.at[:, cols], xv.at[f, :, mine], xf_sem.at[way, q])

    first_copy(0, 0).start()
    first_copy(1, 0).start()
    state_in = [
        pltpu.make_async_copy(m_hbm, mv, in_sem.at[1]),
        pltpu.make_async_copy(c1_hbm, st.at[:, 1], in_sem.at[2]),
        pltpu.make_async_copy(c2_hbm, st.at[:, 2], in_sem.at[3]),
        pltpu.make_async_copy(s1_hbm, sc.at[pl.ds(0, NB)], in_sem.at[4]),
        pltpu.make_async_copy(s2_hbm, sc.at[pl.ds(NB, NB)], in_sem.at[5]),
    ]
    rest = [chunk(yh, (z + 5) % NZ), chunk(y_other, (z + 3) % NZ)]
    for d in (2, 6, 1, 7, 0):
        rest += [chunk(y_other, (z + d) % NZ), chunk(yh, (z + d) % NZ)]

    barrier = pltpu.get_barrier_semaphore()
    for d in (up, down, across):
        pl.semaphore_signal(barrier, inc=1, device_id=d, device_id_type=MESH)

    def greet(r, _):
        pl.semaphore_signal(barrier, inc=1, device_id=(member(r), f_me), device_id_type=MESH)
        return 0

    lax.fori_loop(1, NG, greet, 0)
    for q in range(1, Q):
        first_copy(0, q).start()
        first_copy(1, q).start()
    for f in first_chunks[2:] + rest[:2]:
        x_copy(f).start()
    for c in state_in:
        c.start()
    for f in rest[2:]:
        x_copy(f).start()

    def partial_grad(f, q):
        cols = pl.ds(pl.multiple_of(q * R, R), R)
        return lax.dot_general(
            xv[f, :, cols], cv[...], (((0,), (0,)), ((), ())), preferred_element_type=F32
        )

    def ring_copy(way, n, rows=R):
        part = pl.ds(0, rows)
        return pltpu.make_async_remote_copy(
            src_ref=sbuf.at[way, n, part], dst_ref=rbuf.at[way, n, part],
            send_sem=zs_sem.at[way, n], recv_sem=zr_sem.at[way, n],
            device_id=(up, down)[way], device_id_type=MESH,
        )

    plane_order = (4, 3, 5, 2, 6, 1, 7, 0)

    def plane_copy(i):
        return pltpu.make_async_remote_copy(
            src_ref=ybs.at[i], dst_ref=ybr.at[i], send_sem=bs_sem.at[i], recv_sem=br_sem.at[i],
            device_id=across, device_id_type=MESH,
        )

    def plane_send(i):
        t = (z + plane_order[i]) % NZ
        ybs[i] = partial_grad(chunk(y_other, t), QB)[RO:].astype(BF16)
        plane_copy(i).start()

    def from_plane(i):
        plane_copy(i).wait_recv()
        return ybr[i].astype(F32)

    def slot(d, own, q):
        return (d - 1) * (2 * Q) + own * Q + q

    def ring_piece(way, d, own, q, last=False):
        t = (z + d) % NZ if way == 0 else (z + NZ - d) % NZ
        total = partial_grad(chunk(yh if own else y_other, t), q)
        n = slot(d, own, q)
        rows = RO if last and not own else R
        total = total[:rows]
        if d < 3 or (d == 3 and own == way):
            prev = slot(d + 1, own, q)
            ring_copy(way, prev, rows).wait_recv()
            total = total + rbuf[way, prev, :rows].astype(F32)
        if last and own:
            i = 7 - 2 * d if way == 0 else 8 - 2 * d
            sbuf[way, n, :RO] = total[:RO].astype(BF16)
            sbuf[way, n, RO:] = (total[RO:] + from_plane(i)).astype(BF16)
        else:
            sbuf[way, n, :rows] = total.astype(BF16)
        ring_copy(way, n, rows).start()

    def ring_pieces(d, own_up, own_down, begin=0):
        def body(q, _):
            ring_piece(0, d, own_up, q)
            ring_piece(1, d, own_down, q)
            return 0

        lax.fori_loop(begin, QB, body, 0)
        ring_piece(0, d, own_up, QB, True)
        ring_piece(1, d, own_down, QB, True)

    c_in.wait()
    first_copy(0, 0).wait()
    first_copy(1, 0).wait()
    pl.semaphore_wait(barrier, NG + 2)
    ring_piece(0, 4, 0, 0)
    ring_piece(1, 4, 1, 0)
    for q in range(1, Q):
        first_copy(0, q).wait()
        first_copy(1, q).wait()
    plane_send(0)
    ring_pieces(4, 0, 1, begin=1)
    for f in first_chunks[2:] + rest[:2]:
        x_copy(f).wait()
    plane_send(1)
    plane_send(2)
    ring_pieces(3, 1, 0)
    for f in rest[2:]:
        x_copy(f).wait()
    for i in range(3, NZ):
        plane_send(i)

    for c in state_in:
        c.wait()

    def to_bf16(j, _):
        st[j, 0] = mv[j].astype(BF16)
        return 0

    lax.fori_loop(0, NG, to_bf16, 0)

    def spread_copy(r, src, dst, s_sem, r_sem):
        return pltpu.make_async_remote_copy(
            src_ref=src, dst_ref=dst, send_sem=s_sem, recv_sem=r_sem,
            device_id=(member(r), f_me), device_id_type=MESH,
        )

    def state_out(r):
        return spread_copy(r, st.at[member(r)], st_r.at[g], ss_sem.at[r], sr_sem.at[r])

    def scale_out(r):
        return spread_copy(r, sc, sc_all.at[g], cs_sem.at[r], cr_sem.at[r])

    def state_back(r):
        return spread_copy(r, st_b.at[member(r)], st_p.at[g], ps_sem.at[r], pr_sem.at[r])

    def each_member(fn):
        def body(r, _):
            fn(r)
            return 0

        lax.fori_loop(1, NG, body, 0)

    def start_state(r):
        state_out(r).start()
        scale_out(r).start()

    each_member(start_state)
    st_r[g] = st[g]
    sc_all[g] = sc[...]

    ring_pieces(3, 0, 1)
    ring_pieces(2, 1, 0)

    def state_arrived(r):
        state_out(r).wait_recv()
        scale_out(r).wait_recv()

    each_member(state_arrived)

    def select_state(h, _):
        st_b[h] = st_r[partner_ref[h]]
        return 0

    lax.fori_loop(0, NG, select_state, 0)
    each_member(lambda r: state_back(r).start())
    st_p[g] = st_b[g]

    ring_pieces(2, 0, 1)

    def prepare(who, buf):
        def body(j, _):
            rows = pl.ds(pl.multiple_of(j * SR, SR), SR)
            s = srow[who, rows, :]
            for b in range(NB):
                lanes = slice(b * BLK, (b + 1) * BLK)
                f1[who, rows, lanes] = beta_one * (buf[j, 1, :, lanes].astype(F32) * s[:, b : b + 1])
                f2[who, rows, lanes] = beta_two * (
                    buf[j, 2, :, lanes].astype(F32) * s[:, NB + b : NB + b + 1]
                )
            if who == 1:
                mm[rows, :] = (0.5 * (1.0 - learn_rate * decay_rate)) * (mv[j] + buf[j, 0].astype(F32))
            return 0

        lax.fori_loop(0, NG, body, 0)

    srow[0] = jnp.transpose(sc[...])
    srow[1] = jnp.transpose(sc_all[partner_ref[g]])
    prepare(0, st)
    ring_pieces(1, 0, 0)
    ring_pieces(1, 1, 1)

    def across_copy(q, rows=R):
        part = pl.ds(0, rows)
        return pltpu.make_async_remote_copy(
            src_ref=ysb.at[q, part], dst_ref=yrb.at[q, part],
            send_sem=ys_sem.at[q], recv_sem=yr_sem.at[q], device_id=across, device_id_type=MESH,
        )

    def plane_sum(own, q, rows):
        n = slot(1, own, q)
        total = partial_grad(chunk(yh if own else y_other, z), q)[:rows]
        ring_copy(0, n, rows).wait_recv()
        ring_copy(1, n, rows).wait_recv()
        return total + rbuf[0, n, :rows].astype(F32) + rbuf[1, n, :rows].astype(F32)

    def other_plane(q, rows):
        ysb[q, :rows] = plane_sum(0, q, rows).astype(BF16)
        across_copy(q, rows).start()

    def whole_piece(q, _):
        other_plane(q, R)
        return 0

    lax.fori_loop(0, QB, whole_piece, 0)
    other_plane(QB, RO)
    each_member(lambda r: state_back(r).wait_recv())
    prepare(1, st_p)

    gr = (gr0, gr1, gr2, gr3)

    def grad_out(k, r):
        return spread_copy(r, gs.at[k, member(r)], gr[k].at[g], gs_sem.at[k, r], gr_sem.at[k, r])

    def grad_back(k, r):
        return spread_copy(r, gb.at[k, member(r)], gp.at[k, g], hs_sem.at[k, r], hr_sem.at[k, r])

    def own_plane(q):
        total = plane_sum(1, q, R)
        rows = RO if q == QB else R
        across_copy(q, rows).wait_recv()
        grad[q * R : q * R + rows, :] = total[:rows] + yrb[q, :rows].astype(F32)
        if q == QB:
            grad[W - RB :, :] = total[RO:] + from_plane(7)
        total = grad[q * R : (q + 1) * R, :]
        sent = total.astype(BF16)
        for j in range(NG):
            i, h = j // 2, j % 2
            gs[q, j] = sent[i * MR : (i + 1) * MR, h * HW : (h + 1) * HW]

    def moments(value, who, rows, lanes):
        first = f1[who, rows, lanes] + (1.0 - beta_one) * value
        second = f2[who, rows, lanes] + (1.0 - beta_two) * value * value
        step = first / (jnp.sqrt(second) + adam_epsilon)
        return rounded(first), rounded(second), step

    def quantize(values):
        scale = jnp.max(jnp.abs(values), axis=-1, keepdims=True) + block_epsilon
        return (values * (1.0 / scale)).astype(BF16), scale

    def rounded(values):
        codes, scale = quantize(values)
        return codes.astype(F32) * scale

    def own_update(k):
        def body(i, _):
            rows = pl.ds(pl.multiple_of(k * R + i * TR, TR), TR)
            for b in range(NB):
                lanes = slice(b * BLK, (b + 1) * BLK)
                one, two, step = moments(grad[rows, lanes], 0, rows, lanes)
                mid1[rows, lanes] = one
                mid2[rows, lanes] = two
                upd[rows, lanes] = mm[rows, lanes] - (0.5 * learn_rate) * step
            return 0

        lax.fori_loop(0, R // TR, body, 0)

    def final_update(k):
        def body(i, _):
            rows = pl.ds(pl.multiple_of(k * R + i * TR, TR), TR)
            for b in range(NB):
                lanes = slice(b * BLK, (b + 1) * BLK)
                h, first = b // 2, (b % 2) * BLK
                other = jnp.concatenate(
                    [
                        gp[k, 2 * (i * (TR // MR) + u) + h, :, first : first + BLK]
                        for u in range(TR // MR)
                    ],
                    axis=0,
                )
                one, two, step = moments(other.astype(F32), 1, rows, lanes)
                mo[rows, lanes] = upd[rows, lanes] - (0.5 * learn_rate) * step
                codes, scale = quantize(0.5 * (mid1[rows, lanes] + one))
                c1o[rows, lanes] = codes
                srow[0, rows, b : b + 1] = scale
                codes, scale = quantize(0.5 * (mid2[rows, lanes] + two))
                c2o[rows, lanes] = codes
                srow[0, rows, NB + b : NB + b + 1] = scale
            return 0

        lax.fori_loop(0, R // TR, body, 0)

    def start_grads(k):
        each_member(lambda r: grad_out(k, r).start())
        gr[k][g] = gs[k, g]

    def pass_grads(k):
        each_member(lambda r: grad_out(k, r).wait_recv())

        def select(h, _):
            gb[k, h] = gr[k][partner_ref[h]]
            return 0

        lax.fori_loop(0, NG, select, 0)
        each_member(lambda r: grad_back(k, r).start())
        gp[k, g] = gb[k, g]

    def outs(k):
        rows = pl.ds(k * R, R)
        return [
            pltpu.make_async_copy(mo.at[rows], mo_hbm.at[rows], out_sem.at[k, 0]),
            pltpu.make_async_copy(c1o.at[rows], c1o_hbm.at[rows], out_sem.at[k, 1]),
            pltpu.make_async_copy(c2o.at[rows], c2o_hbm.at[rows], out_sem.at[k, 2]),
        ]

    def finish(k):
        each_member(lambda r: grad_back(k, r).wait_recv())
        final_update(k)
        for c in outs(k):
            c.start()

    def ring_sent(way, d, own):
        def body(q, _):
            ring_copy(way, slot(d, own, q)).wait_send()
            return 0

        lax.fori_loop(0, QB, body, 0)
        ring_copy(way, slot(d, own, QB), R if own else RO).wait_send()

    def planes_sent(i, _):
        plane_copy(i).wait_send()
        return 0

    def across_sent(q, _):
        across_copy(q).wait_send()
        return 0

    def early_sent(r):
        state_out(r).wait_send()
        scale_out(r).wait_send()
        state_back(r).wait_send()

    for k in range(Q):
        own_plane(k)
        start_grads(k)
        own_update(k)
        if k >= 1:
            pass_grads(k - 1)
        if k >= 2:
            finish(k - 2)
    each_member(early_sent)
    lax.fori_loop(0, QB, across_sent, 0)
    across_copy(QB, RO).wait_send()
    lax.fori_loop(0, NZ, planes_sent, 0)
    pass_grads(Q - 1)
    finish(Q - 2)
    for d in (4, 3, 2, 1):
        for own in (0, 1):
            for way in (0, 1):
                if d < 4 or own == way:
                    ring_sent(way, d, own)
    finish(Q - 1)
    so[...] = jnp.transpose(srow[0])
    scale_copies = [
        pltpu.make_async_copy(so.at[pl.ds(0, NB)], so1_hbm, in_sem.at[4]),
        pltpu.make_async_copy(so.at[pl.ds(NB, NB)], so2_hbm, in_sem.at[5]),
    ]
    for c in scale_copies:
        c.start()

    def grads_sent(r):
        for k in range(Q):
            grad_out(k, r).wait_send()
            grad_back(k, r).wait_send()

    each_member(grads_sent)
    for k in range(Q):
        for c in outs(k):
            c.wait()
    for c in scale_copies:
        c.wait()


def store_kernel(*refs):
    ins, outs, sems = refs[:5], refs[5:10], refs[10]
    copies = [pltpu.make_async_copy(a, b, sems.at[i]) for i, (a, b) in enumerate(zip(ins, outs))]
    for c in copies:
        c.start()
    for c in copies:
        c.wait()


def per_device(x, c, master, c1, s1, c2, s2, partner):
    anywhere = pl.BlockSpec(memory_space=pl.ANY)
    in_hbm = pl.BlockSpec(memory_space=pltpu.HBM)
    vm, dma = pltpu.VMEM, pltpu.SemaphoreType.DMA
    results = pl.pallas_call(
        kernel,
        out_shape=(
            jax.ShapeDtypeStruct((W, W), F32),
            jax.ShapeDtypeStruct((W, W), BF16),
            jax.ShapeDtypeStruct((NB, W), F32),
            jax.ShapeDtypeStruct((W, W), BF16),
            jax.ShapeDtypeStruct((NB, W), F32),
        ),
        in_specs=[pl.BlockSpec(memory_space=pltpu.SMEM)] + [in_hbm] * 7,
        out_specs=[anywhere] * 5,
        scratch_shapes=[
            vm((2 * NZ, T, W), BF16), vm((T, W), BF16), vm((NG, SR, W), F32),
            vm((2, SLOTS, R, W), BF16), vm((2, SLOTS, R, W), BF16), vm((Q, R, W), BF16), vm((Q, R, W), BF16),
            vm((NZ, RB, W), BF16), vm((NZ, RB, W), BF16),
            vm((NG, 3, SR, W), BF16), vm((NG, 3, SR, W), BF16), vm((NG, 3, SR, W), BF16),
            vm((NG, 3, SR, W), BF16), vm((2 * NB, W), F32), vm((NG, 2 * NB, W), F32),
            vm((2, W, 2 * NB), F32),
            vm((2, W, W), F32), vm((2, W, W), F32), vm((W, W), F32), vm((W, W), F32),
            vm((Q, NG, MR, HW), BF16), *(vm((NG, MR, HW), BF16) for _ in range(4)),
            vm((Q, NG, MR, HW), BF16), vm((Q, NG, MR, HW), BF16),
            vm((W, W), F32), vm((W, W), F32), vm((W, W), F32),
            vm((W, W), F32), vm((W, W), BF16), vm((W, W), BF16), vm((2 * NB, W), F32),
            dma((2 * NZ,)), dma((2, Q)), dma((6,)), dma((Q, 3)),
            dma((2, SLOTS)), dma((2, SLOTS)), dma((Q,)), dma((Q,)), dma((NZ,)), dma((NZ,)),
            dma((NG,)), dma((NG,)), dma((NG,)), dma((NG,)), dma((NG,)), dma((NG,)),
            dma((Q, NG)), dma((Q, NG)), dma((Q, NG)), dma((Q, NG)),
        ],
        compiler_params=pltpu.CompilerParams(
            collective_id=0, has_side_effects=True, vmem_limit_bytes=50 << 20
        ),
    )(
        pltpu.with_memory_space_constraint(partner, pltpu.SMEM), *(
            pltpu.with_memory_space_constraint(a, pltpu.HBM)
            for a in (
                x[0], c[0], master.reshape(NG, SR, W), c1.reshape(NG, SR, W),
                c2.reshape(NG, SR, W), s1[0].T, s2[0].T,
            )
        )
    )
    mo, c1o, so1, c2o, so2 = pl.pallas_call(
        store_kernel,
        out_shape=tuple(jax.ShapeDtypeStruct(a.shape, a.dtype) for a in results),
        in_specs=[anywhere] * 5,
        out_specs=[in_hbm] * 5,
        scratch_shapes=[dma((5,))],
        compiler_params=pltpu.CompilerParams(vmem_limit_bytes=1 << 20),
    )(*results)
    return (mo[None], c1o[None], so1.T[None], c2o[None], so2.T[None])


def solution(mesh):
    rows = P("group", "fsdp", None)
    return jax.shard_map(
        per_device, mesh=mesh, in_specs=(rows,) * 7 + (P(),), out_specs=(rows,) * 5, check_vma=False
    )
```

```python
import jax
import jax.numpy as jnp
from jax import lax
from jax.experimental import pallas as pl
from jax.experimental.pallas import tpu as pltpu
from jax.sharding import PartitionSpec as P

beta_one = 0.9
beta_two = 0.95
learn_rate = 0.01
decay_rate = 0.1
adam_epsilon = 1e-08
block_epsilon = 1e-06

NG = 16
NZ = 8
T = 384
W = 512
Q = 4
R = W // Q
QB = Q - 1
RB = 80
RO = R - RB
SLOTS = 8 * Q
MR = 2 * R // NG
HW = W // 2
TR = 32
SR = W // NG
BLK = 128
NB = W // BLK
MESH = pl.DeviceIdType.MESH
F32 = jnp.float32
BF16 = jnp.bfloat16


def kernel(
    partner_hbm, x_hbm, c_hbm, m_hbm, c1_hbm, c2_hbm, s1_hbm, s2_hbm,
    mo, c1o, so1, c2o, so2,
    xv, cv, mv, sbuf, rbuf, ysb, yrb, ybs, ybr,
    st, st_r, st_b, st_p, sc, sc_all, srow,
    f1, f2, mm, grad, gs, gr0, gr1, gr2, gr3, gb, gp, mid1, mid2, upd,
    partner_ref, x_sem, xf_sem, in_sem, zs_sem, zr_sem, ys_sem, yr_sem, bs_sem, br_sem,
    ss_sem, sr_sem, cs_sem, cr_sem, ps_sem, pr_sem, gs_sem, gr_sem, hs_sem, hr_sem,
):
    g = lax.axis_index("group")
    f_me = lax.axis_index("fsdp")
    z = f_me % NZ
    yh = f_me // NZ
    y_other = 1 - yh
    up = (g, yh * NZ + (z + 1) % NZ)
    down = (g, yh * NZ + (z + NZ - 1) % NZ)
    across = (g, y_other * NZ + z)

    def member(r):
        return (g + r) % NG

    def x_copy(f):
        cols = pl.ds(pl.multiple_of(f * W, W), W)
        return pltpu.make_async_copy(x_hbm.at[:, cols], xv.at[f], x_sem.at[f])

    def chunk(y, t):
        return y * NZ + t

    far = (z + 4) % NZ
    first_chunks = [
        chunk(y_other, far), chunk(yh, far),
        chunk(yh, (z + 3) % NZ), chunk(y_other, (z + 5) % NZ),
    ]
    c_in = pltpu.make_async_copy(c_hbm, cv, in_sem.at[0])
    c_in.start()

    def first_copy(way, q):
        f = first_chunks[way]
        cols = pl.ds(pl.multiple_of(f * W + q * R, R), R)
        mine = pl.ds(pl.multiple_of(q * R, R), R)
        return pltpu.make_async_copy(x_hbm.at[:, cols], xv.at[f, :, mine], xf_sem.at[way, q])

    first_copy(0, 0).start()
    first_copy(1, 0).start()
    state_in = [
        pltpu.make_async_copy(m_hbm, mv, in_sem.at[1]),
        pltpu.make_async_copy(c1_hbm, st.at[:, 1], in_sem.at[2]),
        pltpu.make_async_copy(c2_hbm, st.at[:, 2], in_sem.at[3]),
        pltpu.make_async_copy(s1_hbm, sc.at[pl.ds(0, NB)], in_sem.at[4]),
        pltpu.make_async_copy(s2_hbm, sc.at[pl.ds(NB, NB)], in_sem.at[5]),
        pltpu.make_async_copy(partner_hbm, partner_ref, in_sem.at[6]),
    ]
    rest = [chunk(yh, (z + 5) % NZ), chunk(y_other, (z + 3) % NZ)]
    for d in (2, 6, 1, 7, 0):
        rest += [chunk(y_other, (z + d) % NZ), chunk(yh, (z + d) % NZ)]

    barrier = pltpu.get_barrier_semaphore()
    for d in (up, down, across):
        pl.semaphore_signal(barrier, inc=1, device_id=d, device_id_type=MESH)

    def greet(r, _):
        pl.semaphore_signal(barrier, inc=1, device_id=(member(r), f_me), device_id_type=MESH)
        return 0

    lax.fori_loop(1, NG, greet, 0)
    for q in range(1, Q):
        first_copy(0, q).start()
        first_copy(1, q).start()
    for f in first_chunks[2:] + rest[:2]:
        x_copy(f).start()
    for c in state_in:
        c.start()
    for f in rest[2:]:
        x_copy(f).start()

    def partial_grad(f, q):
        cols = pl.ds(pl.multiple_of(q * R, R), R)
        return lax.dot_general(
            xv[f, :, cols], cv[...], (((0,), (0,)), ((), ())), preferred_element_type=F32
        )

    def ring_copy(way, n, rows=R):
        part = pl.ds(0, rows)
        return pltpu.make_async_remote_copy(
            src_ref=sbuf.at[way, n, part], dst_ref=rbuf.at[way, n, part],
            send_sem=zs_sem.at[way, n], recv_sem=zr_sem.at[way, n],
            device_id=(up, down)[way], device_id_type=MESH,
        )

    plane_order = (4, 3, 5, 2, 6, 1, 7, 0)

    def plane_copy(i):
        return pltpu.make_async_remote_copy(
            src_ref=ybs.at[i], dst_ref=ybr.at[i], send_sem=bs_sem.at[i], recv_sem=br_sem.at[i],
            device_id=across, device_id_type=MESH,
        )

    def plane_send(i):
        t = (z + plane_order[i]) % NZ
        ybs[i] = partial_grad(chunk(y_other, t), QB)[RO:].astype(BF16)
        plane_copy(i).start()

    def from_plane(i):
        plane_copy(i).wait_recv()
        return ybr[i].astype(F32)

    def slot(d, own, q):
        return (d - 1) * (2 * Q) + own * Q + q

    def ring_piece(way, d, own, q, last=False):
        t = (z + d) % NZ if way == 0 else (z + NZ - d) % NZ
        total = partial_grad(chunk(yh if own else y_other, t), q)
        n = slot(d, own, q)
        rows = RO if last and not own else R
        total = total[:rows]
        if d < 3 or (d == 3 and own == way):
            prev = slot(d + 1, own, q)
            ring_copy(way, prev, rows).wait_recv()
            total = total + rbuf[way, prev, :rows].astype(F32)
        if last and own:
            i = 7 - 2 * d if way == 0 else 8 - 2 * d
            sbuf[way, n, :RO] = total[:RO].astype(BF16)
            sbuf[way, n, RO:] = (total[RO:] + from_plane(i)).astype(BF16)
        else:
            sbuf[way, n, :rows] = total.astype(BF16)
        ring_copy(way, n, rows).start()

    def ring_pieces(d, own_up, own_down, begin=0):
        def body(q, _):
            ring_piece(0, d, own_up, q)
            ring_piece(1, d, own_down, q)
            return 0

        lax.fori_loop(begin, QB, body, 0)
        ring_piece(0, d, own_up, QB, True)
        ring_piece(1, d, own_down, QB, True)

    c_in.wait()
    first_copy(0, 0).wait()
    first_copy(1, 0).wait()
    pl.semaphore_wait(barrier, NG + 2)
    ring_piece(0, 4, 0, 0)
    ring_piece(1, 4, 1, 0)
    for q in range(1, Q):
        first_copy(0, q).wait()
        first_copy(1, q).wait()
    plane_send(0)
    ring_pieces(4, 0, 1, begin=1)
    for f in first_chunks[2:] + rest[:2]:
        x_copy(f).wait()
    plane_send(1)
    plane_send(2)
    ring_pieces(3, 1, 0)
    for f in rest[2:]:
        x_copy(f).wait()
    for i in range(3, NZ):
        plane_send(i)

    for c in state_in:
        c.wait()

    def to_bf16(j, _):
        st[j, 0] = mv[j].astype(BF16)
        return 0

    lax.fori_loop(0, NG, to_bf16, 0)

    def spread_copy(r, src, dst, s_sem, r_sem):
        return pltpu.make_async_remote_copy(
            src_ref=src, dst_ref=dst, send_sem=s_sem, recv_sem=r_sem,
            device_id=(member(r), f_me), device_id_type=MESH,
        )

    def state_out(r):
        return spread_copy(r, st.at[member(r)], st_r.at[g], ss_sem.at[r], sr_sem.at[r])

    def scale_out(r):
        return spread_copy(r, sc, sc_all.at[g], cs_sem.at[r], cr_sem.at[r])

    def state_back(r):
        return spread_copy(r, st_b.at[member(r)], st_p.at[g], ps_sem.at[r], pr_sem.at[r])

    def each_member(fn):
        def body(r, _):
            fn(r)
            return 0

        lax.fori_loop(1, NG, body, 0)

    def start_state(r):
        state_out(r).start()
        scale_out(r).start()

    each_member(start_state)
    st_r[g] = st[g]
    sc_all[g] = sc[...]

    ring_pieces(3, 0, 1)
    ring_pieces(2, 1, 0)

    ring_pieces(2, 0, 1)

    def state_arrived(r):
        state_out(r).wait_recv()
        scale_out(r).wait_recv()

    each_member(state_arrived)

    def select_state(h, _):
        st_b[h] = st_r[partner_ref[h]]
        return 0

    lax.fori_loop(0, NG, select_state, 0)
    each_member(lambda r: state_back(r).start())
    st_p[g] = st_b[g]


    def prepare(who, buf):
        def body(j, _):
            rows = pl.ds(pl.multiple_of(j * SR, SR), SR)
            s = srow[who, rows, :]
            for b in range(NB):
                lanes = slice(b * BLK, (b + 1) * BLK)
                f1[who, rows, lanes] = beta_one * (buf[j, 1, :, lanes].astype(F32) * s[:, b : b + 1])
                f2[who, rows, lanes] = beta_two * (
                    buf[j, 2, :, lanes].astype(F32) * s[:, NB + b : NB + b + 1]
                )
            if who == 1:
                mm[rows, :] = (0.5 * (1.0 - learn_rate * decay_rate)) * (mv[j] + buf[j, 0].astype(F32))
            return 0

        lax.fori_loop(0, NG, body, 0)

    srow[0] = jnp.transpose(sc[...])
    srow[1] = jnp.transpose(sc_all[partner_ref[g]])
    prepare(0, st)
    ring_pieces(1, 0, 0)
    ring_pieces(1, 1, 1)

    def across_copy(q, rows=R):
        part = pl.ds(0, rows)
        return pltpu.make_async_remote_copy(
            src_ref=ysb.at[q, part], dst_ref=yrb.at[q, part],
            send_sem=ys_sem.at[q], recv_sem=yr_sem.at[q], device_id=across, device_id_type=MESH,
        )

    def plane_sum(own, q, rows):
        n = slot(1, own, q)
        total = partial_grad(chunk(yh if own else y_other, z), q)[:rows]
        ring_copy(0, n, rows).wait_recv()
        ring_copy(1, n, rows).wait_recv()
        return total + rbuf[0, n, :rows].astype(F32) + rbuf[1, n, :rows].astype(F32)

    def other_plane(q, rows):
        ysb[q, :rows] = plane_sum(0, q, rows).astype(BF16)
        across_copy(q, rows).start()

    def whole_piece(q, _):
        other_plane(q, R)
        return 0

    lax.fori_loop(0, QB, whole_piece, 0)
    other_plane(QB, RO)
    each_member(lambda r: state_back(r).wait_recv())
    prepare(1, st_p)

    gr = (gr0, gr1, gr2, gr3)

    def grad_out(k, r):
        return spread_copy(r, gs.at[k, member(r)], gr[k].at[g], gs_sem.at[k, r], gr_sem.at[k, r])

    def grad_back(k, r):
        return spread_copy(r, gb.at[k, member(r)], gp.at[k, g], hs_sem.at[k, r], hr_sem.at[k, r])

    def own_plane(q):
        total = plane_sum(1, q, R)
        rows = RO if q == QB else R
        across_copy(q, rows).wait_recv()
        grad[q * R : q * R + rows, :] = total[:rows] + yrb[q, :rows].astype(F32)
        if q == QB:
            grad[W - RB :, :] = total[RO:] + from_plane(7)
        total = grad[q * R : (q + 1) * R, :]
        sent = total.astype(BF16)
        for j in range(NG):
            i, h = j // 2, j % 2
            gs[q, j] = sent[i * MR : (i + 1) * MR, h * HW : (h + 1) * HW]

    def moments(value, who, rows, lanes):
        first = f1[who, rows, lanes] + (1.0 - beta_one) * value
        second = f2[who, rows, lanes] + (1.0 - beta_two) * value * value
        step = first / (jnp.sqrt(second) + adam_epsilon)
        return rounded(first), rounded(second), step

    def quantize(values):
        scale = jnp.max(jnp.abs(values), axis=-1, keepdims=True) + block_epsilon
        return (values * (1.0 / scale)).astype(BF16), scale

    def rounded(values):
        codes, scale = quantize(values)
        return codes.astype(F32) * scale

    def own_update(k):
        def body(i, _):
            rows = pl.ds(pl.multiple_of(k * R + i * TR, TR), TR)
            for b in range(NB):
                lanes = slice(b * BLK, (b + 1) * BLK)
                one, two, step = moments(grad[rows, lanes], 0, rows, lanes)
                mid1[rows, lanes] = one
                mid2[rows, lanes] = two
                upd[rows, lanes] = mm[rows, lanes] - (0.5 * learn_rate) * step
            return 0

        lax.fori_loop(0, R // TR, body, 0)

    def final_update(k):
        def body(i, _):
            rows = pl.ds(pl.multiple_of(k * R + i * TR, TR), TR)
            for b in range(NB):
                lanes = slice(b * BLK, (b + 1) * BLK)
                h, first = b // 2, (b % 2) * BLK
                other = jnp.concatenate(
                    [
                        gp[k, 2 * (i * (TR // MR) + u) + h, :, first : first + BLK]
                        for u in range(TR // MR)
                    ],
                    axis=0,
                )
                one, two, step = moments(other.astype(F32), 1, rows, lanes)
                mo[rows, lanes] = upd[rows, lanes] - (0.5 * learn_rate) * step
                codes, scale = quantize(0.5 * (mid1[rows, lanes] + one))
                c1o[rows, lanes] = codes
                srow[0, rows, b : b + 1] = scale
                codes, scale = quantize(0.5 * (mid2[rows, lanes] + two))
                c2o[rows, lanes] = codes
                srow[0, rows, NB + b : NB + b + 1] = scale
            return 0

        lax.fori_loop(0, R // TR, body, 0)

    def start_grads(k):
        each_member(lambda r: grad_out(k, r).start())
        gr[k][g] = gs[k, g]

    def pass_grads(k):
        each_member(lambda r: grad_out(k, r).wait_recv())

        def select(h, _):
            gb[k, h] = gr[k][partner_ref[h]]
            return 0

        lax.fori_loop(0, NG, select, 0)
        each_member(lambda r: grad_back(k, r).start())
        gp[k, g] = gb[k, g]

    def finish(k):
        each_member(lambda r: grad_back(k, r).wait_recv())
        final_update(k)

    def ring_sent(way, d, own):
        def body(q, _):
            ring_copy(way, slot(d, own, q)).wait_send()
            return 0

        lax.fori_loop(0, QB, body, 0)
        ring_copy(way, slot(d, own, QB), R if own else RO).wait_send()

    def planes_sent(i, _):
        plane_copy(i).wait_send()
        return 0

    def across_sent(q, _):
        across_copy(q).wait_send()
        return 0

    def early_sent(r):
        state_out(r).wait_send()
        scale_out(r).wait_send()
        state_back(r).wait_send()

    for k in range(Q):
        own_plane(k)
        start_grads(k)
        if k >= 1:
            pass_grads(k - 1)
        own_update(k)
        if 2 <= k < Q - 1:
            finish(k - 2)
    pass_grads(Q - 1)
    each_member(early_sent)
    lax.fori_loop(0, QB, across_sent, 0)
    across_copy(QB, RO).wait_send()
    lax.fori_loop(0, NZ, planes_sent, 0)
    finish(Q - 3)
    finish(Q - 2)
    for d in (4, 3, 2, 1):
        for own in (0, 1):
            for way in (0, 1):
                if d < 4 or own == way:
                    ring_sent(way, d, own)
    finish(Q - 1)
    scales = jnp.transpose(srow[0])
    so1[...] = scales[:NB]
    so2[...] = scales[NB:]

    def grads_sent(r):
        for k in range(Q):
            grad_out(k, r).wait_send()
            grad_back(k, r).wait_send()

    each_member(grads_sent)


def store_kernel(*refs):
    ins, outs, sems = refs[:5], refs[5:10], refs[10]
    copies = [pltpu.make_async_copy(a, b, sems.at[i]) for i, (a, b) in enumerate(zip(ins, outs))]
    for c in copies:
        c.start()
    for c in copies:
        c.wait()


def per_device(x, c, master, c1, s1, c2, s2, partner):
    anywhere = pl.BlockSpec(memory_space=pl.ANY)
    in_hbm = pl.BlockSpec(memory_space=pltpu.HBM)
    vm, dma = pltpu.VMEM, pltpu.SemaphoreType.DMA
    results = pl.pallas_call(
        kernel,
        out_shape=(
            jax.ShapeDtypeStruct((W, W), F32),
            jax.ShapeDtypeStruct((W, W), BF16),
            jax.ShapeDtypeStruct((NB, W), F32),
            jax.ShapeDtypeStruct((W, W), BF16),
            jax.ShapeDtypeStruct((NB, W), F32),
        ),
        in_specs=[in_hbm] * 8,
        out_specs=[pl.BlockSpec(memory_space=pltpu.VMEM)] * 5,
        scratch_shapes=[
            vm((2 * NZ, T, W), BF16), vm((T, W), BF16), vm((NG, SR, W), F32),
            vm((2, SLOTS, R, W), BF16), vm((2, SLOTS, R, W), BF16), vm((Q, R, W), BF16), vm((Q, R, W), BF16),
            vm((NZ, RB, W), BF16), vm((NZ, RB, W), BF16),
            vm((NG, 3, SR, W), BF16), vm((NG, 3, SR, W), BF16), vm((NG, 3, SR, W), BF16),
            vm((NG, 3, SR, W), BF16), vm((2 * NB, W), F32), vm((NG, 2 * NB, W), F32),
            vm((2, W, 2 * NB), F32),
            vm((2, W, W), F32), vm((2, W, W), F32), vm((W, W), F32), vm((W, W), F32),
            vm((Q, NG, MR, HW), BF16), *(vm((NG, MR, HW), BF16) for _ in range(4)),
            vm((Q, NG, MR, HW), BF16), vm((Q, NG, MR, HW), BF16),
            vm((W, W), F32), vm((W, W), F32), vm((W, W), F32),
            pltpu.SMEM((NG,), jnp.int32), dma((2 * NZ,)), dma((2, Q)), dma((7,)),
            dma((2, SLOTS)), dma((2, SLOTS)), dma((Q,)), dma((Q,)), dma((NZ,)), dma((NZ,)),
            dma((NG,)), dma((NG,)), dma((NG,)), dma((NG,)), dma((NG,)), dma((NG,)),
            dma((Q, NG)), dma((Q, NG)), dma((Q, NG)), dma((Q, NG)),
        ],
        compiler_params=pltpu.CompilerParams(
            collective_id=0, has_side_effects=True, vmem_limit_bytes=50 << 20
        ),
    )(
        *(
            pltpu.with_memory_space_constraint(a, pltpu.HBM)
            for a in (
                partner, x[0], c[0], master.reshape(NG, SR, W), c1.reshape(NG, SR, W),
                c2.reshape(NG, SR, W), s1[0].T, s2[0].T,
            )
        )
    )
    mo, c1o, so1, c2o, so2 = pl.pallas_call(
        store_kernel,
        out_shape=tuple(jax.ShapeDtypeStruct(a.shape, a.dtype) for a in results),
        in_specs=[anywhere] * 5,
        out_specs=[in_hbm] * 5,
        scratch_shapes=[dma((5,))],
        compiler_params=pltpu.CompilerParams(vmem_limit_bytes=1 << 20),
    )(*results)
    return (mo[None], c1o[None], so1.T[None], c2o[None], so2.T[None])


def solution(mesh):
    rows = P("group", "fsdp", None)
    return jax.shard_map(
        per_device, mesh=mesh, in_specs=(rows,) * 7 + (P(),), out_specs=(rows,) * 5, check_vma=False
    )
```
